512 devices in a mesh: dp: 8 (over y, x_hi), row: 16 (over z), col: 4 (over x_lo, core).
Axes of the slice: x: 4 (x_hi: 2, x_lo: 2; x = x_hi * 2 + x_lo), y: 4, z: 16, core: 2. Of those that a mesh axis runs over, the one named last changes fastest.
Arguments:
- gate_pre: bfloat16 [4096, 14336], P(('dp', 'col'), 'row'), may hold values from -6 to 6
- up_pre: bfloat16 [4096, 14336], P(('dp', 'col'), 'row'), may hold values from -6 to 6
- out_grad: bfloat16 [4096, 4096], P(('dp', 'row'), 'col'), may hold values from -6 to 6
- down_weight: bfloat16 [14336, 4096], P('row', 'col'), may hold values from -0.046875 to 0.046875
Outputs:
- layer_out: bfloat16 [4096, 4096], P(('dp', 'row'), 'col')
- gate_grad: bfloat16 [4096, 14336], P(('dp', 'col'), 'row')
- up_grad: bfloat16 [4096, 14336], P(('dp', 'col'), 'row')
- weight_grad: float32 [14336, 4096], P(('row', 'dp'), 'col')
The draws below stay inside these ranges and needn't reach their ends.
All inputs are finite; a program needn't handle non-finite values.
Results may differ from the reference program's by a relative error of at most 0.017.
Values may be sent and summed in bfloat16 or wider, within the bound.
No kernel may reach another device: no remote copies, remote signals or barrier semaphores. Data moves between devices by JAX's collectives and lax.ppermute only.
A program may use at most 64 MiB of HBM per device.

```python
import jax
import jax.numpy as jnp
from jax import lax

MODEL_HALF = 4096
FF = 14336
REPLICA_TOKENS = 512
TOKENS = 4096
N_DP = 8
N_ROW = 16
N_COL = 4


def strengthened(array, key, source, target, parts, factor):
    owner, partner = [(jnp.arange(array.shape[axis_at]) // (array.shape[axis_at] // parts)).reshape([-1 if axis == axis_at else 1 for axis in range(array.ndim)]) for axis_at in (source, target)]
    chosen = jax.random.permutation(key, parts)[partner]
    strong = (owner == chosen) | (owner == (partner + parts // 2) % parts)
    return jnp.where(strong, factor * array, array)


def shard_levels(own_key, dims, split, low, largest):
    loudness = 1.0
    for axis_at, blocks in split:
        draws = jax.random.uniform(jax.random.fold_in(jax.random.fold_in(own_key, 6), axis_at), (blocks,), jnp.float32, low / len(split), largest / len(split))
        loudness = loudness * jnp.repeat(jnp.exp(draws), dims[axis_at] // blocks).reshape((-1,) + (1,) * (len(dims) - 1 - axis_at))
    return loudness


def normal_values(key, dims, deviation, limit, shards=(), held_as=jnp.bfloat16):
    values = jax.random.normal(key, dims, jnp.float32) * deviation
    if len(shards) > 0:
        values = shard_levels(key, dims, shards, -0.22, 0.18) * values
    return jnp.clip(values, min=-limit, max=limit).astype(held_as)


def bell_draw_with(own_key, extent, spread, reach, pieces, heavy, held_as=jnp.bfloat16):
    drawn = spread * jax.random.normal(own_key, extent, jnp.float32)
    if pieces:
        drawn = drawn * shard_levels(own_key, extent, pieces, -0.22, 0.18)
    return jnp.clip(strengthened(drawn, jax.random.fold_in(own_key, 3), *heavy), -reach, reach).astype(held_as)


def setup_inputs(seed: int = 0) -> dict:
    key_list = jax.random.split(jax.random.key(seed), 5)
    gate_pre = normal_values(key_list[0], (TOKENS, FF), 1.0, 6.0, ((0, 32), (1, 16)))
    up_pre = bell_draw_with(key_list[1], (TOKENS, FF), 1.0, 6.0, ((0, 32), (1, 16)), (0, 1, 32, 2.75))
    out_grad = normal_values(key_list[2], (TOKENS, MODEL_HALF), 1.0, 6.0, ((0, 128), (1, 4)))
    down_weight = normal_values(key_list[3], (FF, MODEL_HALF), FF ** -0.5, 0.046875, ((0, 16), (1, 4)))
    return {"gate_pre": gate_pre, "up_pre": up_pre, "out_grad": out_grad, "down_weight": down_weight}


def rounded(value):
    return lax.optimization_barrier(value.astype(jnp.bfloat16)).astype(jnp.float32)


def reference(gate_pre, up_pre, out_grad, down_weight):
    hidden_block = FF // N_ROW
    feature_block = MODEL_HALF // N_COL
    gate32 = gate_pre.astype(jnp.float32)
    up32 = up_pre.astype(jnp.float32)
    sgate = jax.nn.sigmoid(gate32)
    act = gate32 * sgate
    hidden = (act * up32).astype(jnp.bfloat16)
    hidden_rep = hidden.reshape(N_DP, REPLICA_TOKENS, FF)
    grad_rep = out_grad.reshape(N_DP, REPLICA_TOKENS, MODEL_HALF)
    weight_single = down_weight.astype(jnp.float32)

    def forward(hidden_input):
        partial_terms = jnp.einsum("soe,oel->osl", hidden_input.astype(jnp.float32).reshape(REPLICA_TOKENS, N_ROW, hidden_block), weight_single.reshape(N_ROW, hidden_block, MODEL_HALF))
        return jnp.sum(rounded(partial_terms), axis=0)

    layer_out = lax.map(forward, hidden_rep).reshape(TOKENS, MODEL_HALF).astype(jnp.bfloat16)

    def backward(cot):
        partial_terms = jnp.einsum("tcd,fcd->ctf", cot.astype(jnp.float32).reshape(REPLICA_TOKENS, N_COL, feature_block), weight_single.reshape(FF, N_COL, feature_block))
        return jnp.sum(rounded(partial_terms), axis=0)

    dhidden = lax.map(backward, grad_rep).reshape(TOKENS, FF)
    up_grad = (dhidden * act).astype(jnp.bfloat16)
    gate_grad = (dhidden * up32 * sgate * (1.0 + gate32 * (1.0 - sgate))).astype(jnp.bfloat16)
    factor = 1.0 / (TOKENS ** 0.5)

    def accumulate(total, pair):
        hidden_input, cot = pair
        part = jnp.dot(hidden_input.T, cot, preferred_element_type=jnp.float32) * factor
        return total + rounded(part), None

    weight_grad, unused = lax.scan(accumulate, jnp.zeros((FF, MODEL_HALF), jnp.float32), (hidden_rep, grad_rep))
    return layer_out, gate_grad, up_grad, weight_grad
```

```python
import jax
import jax.numpy as jnp
from jax import lax
from jax.sharding import PartitionSpec as P

hold = lax.optimization_barrier


def exchange_sum(parts, axis):
    count = lax.axis_size(axis)
    parts = parts.reshape((count, parts.shape[0] // count) + parts.shape[1:])
    parts = lax.all_to_all(parts, axis, 0, 0, tiled=True)
    return jnp.sum(parts.astype(jnp.float32), axis=0)


def shards(gate_pre, up_pre, out_grad, down_weight):
    gate32 = gate_pre.astype(jnp.float32)
    up32 = up_pre.astype(jnp.float32)
    sgate = jax.nn.sigmoid(gate32)
    act = gate32 * sgate
    hidden = hold((act * up32).astype(jnp.bfloat16))
    hidden_all = lax.all_gather(hidden, "col", axis=0, tiled=True)
    layer_parts = jnp.dot(hidden_all, down_weight, preferred_element_type=jnp.float32).astype(jnp.bfloat16)
    layer_out = exchange_sum(layer_parts, "row").astype(jnp.bfloat16)

    half = out_grad.shape[1] // 2
    grad_all = jnp.concatenate(
        [
            lax.all_gather(out_grad[:, :half], "row", axis=0, tiled=True),
            lax.all_gather(out_grad[:, half:], "row", axis=0, tiled=True),
        ],
        axis=1,
    )
    hidden_all, grad_all = hold((hidden_all, grad_all))
    dhidden = exchange_sum(
        lax.dot_general(
            grad_all, down_weight, (((1,), (1,)), ((), ())), preferred_element_type=jnp.float32
        ).astype(jnp.bfloat16),
        "col",
    )
    up_grad = (dhidden * act).astype(jnp.bfloat16)
    gate_grad = (dhidden * up32 * sgate * (1.0 + gate32 * (1.0 - sgate))).astype(jnp.bfloat16)
    factor = 1.0 / (hidden_all.shape[0] * lax.axis_size("dp")) ** 0.5
    local_grad = (
        lax.dot_general(
            hidden_all, grad_all, (((0,), (0,)), ((), ())), preferred_element_type=jnp.float32
        )
        * factor
    )
    weight_grad = exchange_sum(local_grad.astype(jnp.bfloat16), "dp")
    return (layer_out, gate_grad, up_grad, weight_grad)


def solution(mesh):
    return jax.shard_map(
        shards,
        mesh=mesh,
        in_specs=(
            P(("dp", "col"), "row"),
            P(("dp", "col"), "row"),
            P(("dp", "row"), "col"),
            P("row", "col"),
        ),
        out_specs=(
            P(("dp", "row"), "col"),
            P(("dp", "col"), "row"),
            P(("dp", "col"), "row"),
            P(("row", "dp"), "col"),
        ),
        check_vma=False,
    )
```

```python
import jax
import jax.numpy as jnp
from jax import lax
from jax.sharding import PartitionSpec as P

hold = lax.optimization_barrier


def shifted(array, axis, by):
    count = lax.axis_size(axis)
    return lax.ppermute(array, axis, [(i, (i + by) % count) for i in range(count)])


def pick(array, index):
    return lax.dynamic_index_in_dim(array, index, 0, keepdims=False)


def gather_rows(block):
    me = lax.axis_index("row")
    high, low = me >> 2, me & 3
    same = jnp.zeros((4,) + block.shape, block.dtype)
    for k in range(4):
        got = block if k == 0 else shifted(block, "row", 4 * k)
        same = lax.dynamic_update_slice(same, got[None], ((high - k) & 3, 0, 0))
    whole = jnp.zeros((4, 4) + block.shape, block.dtype)
    for by in (1, 15, 2, 0):
        got = same if by == 0 else shifted(same, "row", by)
        whole = lax.dynamic_update_slice(whole, got[:, None], (0, (low - by) & 3, 0, 0))
    return whole.reshape(-1, block.shape[-1])


def sum_over_row(parts):
    count = lax.axis_size("row")
    parts = parts.reshape((count, parts.shape[0] // count) + parts.shape[1:])
    parts = lax.all_to_all(parts, "row", 0, 0, tiled=True)
    return jnp.sum(parts.astype(jnp.float32), axis=0)


def sum_over_dp(parts):
    parts = parts.reshape((8, parts.shape[0] // 8) + parts.shape[1:])
    me = lax.axis_index("dp")
    y, x = me >> 1, me & 1
    total = pick(parts, me).astype(jnp.float32)
    for dy, dx in ((1, 0), (3, 0), (0, 1), (1, 1), (3, 1), (2, 0), (2, 1)):
        route = [(a * 2 + b, (a + dy) % 4 * 2 + (b + dx) % 2) for a in range(4) for b in range(2)]
        mine = pick(parts, ((y + dy) & 3) * 2 + ((x + dx) & 1))
        total = total + lax.ppermute(mine, "dp", route).astype(jnp.float32)
    return total


def sum_over_col(parts):
    parts = parts.reshape((2, 2, parts.shape[0] // 4) + parts.shape[1:])
    me = lax.axis_index("col")
    x, core = me >> 1, me & 1
    other = lax.dynamic_index_in_dim(parts, 1 - core, 1, keepdims=False)
    mine = lax.dynamic_index_in_dim(parts, core, 1, keepdims=False)
    other = lax.ppermute(other, "col", [(i, i ^ 1) for i in range(4)])
    pair = mine.astype(jnp.float32) + other.astype(jnp.float32)
    away = lax.ppermute(pick(pair, 1 - x).astype(jnp.bfloat16), "col", [(i, i ^ 2) for i in range(4)])
    return pick(pair, x) + away.astype(jnp.float32)


def shards(gate_pre, up_pre, out_grad, down_weight):
    grad_all = gather_rows(out_grad)

    gate32 = gate_pre.astype(jnp.float32)
    up32 = up_pre.astype(jnp.float32)
    sgate = jax.nn.sigmoid(gate32)
    act = gate32 * sgate
    hidden = hold((act * up32).astype(jnp.bfloat16))
    hidden_all = lax.all_gather(hidden, "col", axis=0, tiled=True)
    layer_parts = jnp.dot(hidden_all, down_weight, preferred_element_type=jnp.float32).astype(jnp.bfloat16)
    layer_out = sum_over_row(layer_parts).astype(jnp.bfloat16)

    hidden_all, grad_all = hold((hidden_all, grad_all))
    factor = 1.0 / (hidden_all.shape[0] * lax.axis_size("dp")) ** 0.5
    local_grad = (
        lax.dot_general(
            hidden_all, grad_all, (((0,), (0,)), ((), ())), preferred_element_type=jnp.float32
        )
        * factor
    )
    weight_grad = sum_over_dp(local_grad.astype(jnp.bfloat16))
    dhidden = sum_over_col(
        lax.dot_general(
            grad_all, down_weight, (((1,), (1,)), ((), ())), preferred_element_type=jnp.float32
        ).astype(jnp.bfloat16)
    )
    up_grad = (dhidden * act).astype(jnp.bfloat16)
    gate_grad = (dhidden * up32 * sgate * (1.0 + gate32 * (1.0 - sgate))).astype(jnp.bfloat16)
    return (layer_out, gate_grad, up_grad, weight_grad)


def solution(mesh):
    return jax.shard_map(
        shards,
        mesh=mesh,
        in_specs=(
            P(("dp", "col"), "row"),
            P(("dp", "col"), "row"),
            P(("dp", "row"), "col"),
            P("row", "col"),
        ),
        out_specs=(
            P(("dp", "row"), "col"),
            P(("dp", "col"), "row"),
            P(("dp", "col"), "row"),
            P(("row", "dp"), "col"),
        ),
        check_vma=False,
    )
```

```python
import jax
import jax.numpy as jnp
from jax import lax
from jax.sharding import PartitionSpec as P

hold = lax.optimization_barrier


def shifted(array, axis, by):
    count = lax.axis_size(axis)
    return lax.ppermute(array, axis, [(i, (i + by) % count) for i in range(count)])


def pick(array, index):
    return lax.dynamic_index_in_dim(array, index, 0, keepdims=False)


def gather_apart(block):
    groups = [[k, k + 4, k + 8, k + 12] for k in range(4)]
    return lax.all_gather(block, "row", axis=0, tiled=False, axis_index_groups=groups)


def gather_near(same):
    low = lax.axis_index("row") & 3
    whole = jnp.zeros((4,) + same.shape, same.dtype)
    for by in (1, 15, 2, 0):
        got = same if by == 0 else shifted(same, "row", by)
        whole = lax.dynamic_update_slice(whole, got[:, None], (0, (low - by) & 3, 0, 0))
    return whole.reshape(-1, same.shape[-1])


def sum_over_row(parts):
    count = lax.axis_size("row")
    parts = parts.reshape((count, parts.shape[0] // count) + parts.shape[1:])
    parts = lax.all_to_all(parts, "row", 0, 0, tiled=True)
    return jnp.sum(parts.astype(jnp.float32), axis=0)


def sum_over_dp(parts):
    parts = parts.reshape((8, parts.shape[0] // 8) + parts.shape[1:])
    me = lax.axis_index("dp")
    y, x = me >> 1, me & 1
    total = pick(parts, me).astype(jnp.float32)
    for dy, dx in ((1, 0), (3, 0), (0, 1), (1, 1), (3, 1), (2, 0), (2, 1)):
        route = [(a * 2 + b, (a + dy) % 4 * 2 + (b + dx) % 2) for a in range(4) for b in range(2)]
        mine = pick(parts, ((y + dy) & 3) * 2 + ((x + dx) & 1))
        total = total + lax.ppermute(mine, "dp", route).astype(jnp.float32)
    return total


def sum_over_col(parts):
    parts = parts.reshape((2, 2, parts.shape[0] // 4) + parts.shape[1:])
    me = lax.axis_index("col")
    x, core = me >> 1, me & 1
    other = lax.dynamic_index_in_dim(parts, 1 - core, 1, keepdims=False)
    mine = lax.dynamic_index_in_dim(parts, core, 1, keepdims=False)
    other = lax.ppermute(other, "col", [(i, i ^ 1) for i in range(4)])
    pair = mine.astype(jnp.float32) + other.astype(jnp.float32)
    away = lax.ppermute(pick(pair, 1 - x).astype(jnp.bfloat16), "col", [(i, i ^ 2) for i in range(4)])
    return pick(pair, x) + away.astype(jnp.float32)


def shards(gate_pre, up_pre, out_grad, down_weight):
    grad_apart = gather_apart(out_grad)

    gate32 = gate_pre.astype(jnp.float32)
    up32 = up_pre.astype(jnp.float32)
    sgate = jax.nn.sigmoid(gate32)
    act = gate32 * sgate
    hidden, grad_apart = hold(((act * up32).astype(jnp.bfloat16), grad_apart))
    grad_all = gather_near(grad_apart)
    hidden_all = lax.all_gather(hidden, "col", axis=0, tiled=True)
    layer_parts = jnp.dot(hidden_all, down_weight, preferred_element_type=jnp.float32).astype(jnp.bfloat16)
    layer_out = sum_over_row(layer_parts).astype(jnp.bfloat16)

    hidden_all, grad_all = hold((hidden_all, grad_all))
    factor = 1.0 / (hidden_all.shape[0] * lax.axis_size("dp")) ** 0.5
    local_grad = (
        lax.dot_general(
            hidden_all, grad_all, (((0,), (0,)), ((), ())), preferred_element_type=jnp.float32
        )
        * factor
    ).astype(jnp.bfloat16)
    local_grad, grad_late = hold((local_grad, grad_all))
    weight_grad = sum_over_dp(local_grad)
    dhidden = sum_over_col(
        lax.dot_general(
            grad_late, down_weight, (((1,), (1,)), ((), ())), preferred_element_type=jnp.float32
        ).astype(jnp.bfloat16)
    )
    up_grad = (dhidden * act).astype(jnp.bfloat16)
    gate_grad = (dhidden * up32 * sgate * (1.0 + gate32 * (1.0 - sgate))).astype(jnp.bfloat16)
    return (layer_out, gate_grad, up_grad, weight_grad)


def solution(mesh):
    return jax.shard_map(
        shards,
        mesh=mesh,
        in_specs=(
            P(("dp", "col"), "row"),
            P(("dp", "col"), "row"),
            P(("dp", "row"), "col"),
            P("row", "col"),
        ),
        out_specs=(
            P(("dp", "row"), "col"),
            P(("dp", "col"), "row"),
            P(("dp", "col"), "row"),
            P(("row", "dp"), "col"),
        ),
        check_vma=False,
    )
```

```python
import jax
import jax.numpy as jnp
from jax import lax
from jax.sharding import PartitionSpec as P

hold = lax.optimization_barrier


def shifted(array, axis, by):
    count = lax.axis_size(axis)
    return lax.ppermute(array, axis, [(i, (i + by) % count) for i in range(count)])


def pick(array, index):
    return lax.dynamic_index_in_dim(array, index, 0, keepdims=False)


def gather_apart(block):
    groups = [[k, k + 4, k + 8, k + 12] for k in range(4)]
    return lax.all_gather(block, "row", axis=0, tiled=False, axis_index_groups=groups)


def gather_near(same):
    low = lax.axis_index("row") & 3
    sets = [same]
    for by in (1, 2, 15):
        sets.append(shifted(same, "row", by))
    whole = [lax.select_n((low - k) & 3, *sets) for k in range(4)]
    return jnp.stack(whole, axis=1).reshape(-1, same.shape[-1])


def sum_over_row(parts):
    count = lax.axis_size("row")
    parts = parts.reshape((count, parts.shape[0] // count) + parts.shape[1:])
    parts = lax.all_to_all(parts, "row", 0, 0, tiled=True)
    return jnp.sum(parts.astype(jnp.float32), axis=0)


def sum_over_dp(parts):
    parts = parts.reshape((4, 2, parts.shape[0] // 8) + parts.shape[1:])
    me = lax.axis_index("dp")
    y, x = me >> 1, me & 1
    own, *blocks = hold([pick(parts, (y + dy) & 3) for dy in (0, 2, 1, 3)])
    total = own.astype(jnp.float32)
    for dy, mine in zip((2, 1, 3), blocks):
        got = lax.ppermute(mine, "dp", [(i, (i + 2 * dy) % 8) for i in range(8)])
        total = total + got.astype(jnp.float32)
    away = pick(total, 1 - x).astype(jnp.bfloat16)
    away = lax.ppermute(away, "dp", [(i, i ^ 1) for i in range(8)])
    return pick(total, x) + away.astype(jnp.float32)


def sum_over_col(parts):
    parts = parts.reshape((2, 2, parts.shape[0] // 4) + parts.shape[1:])
    me = lax.axis_index("col")
    x, core = me >> 1, me & 1
    other = lax.dynamic_index_in_dim(parts, 1 - core, 1, keepdims=False)
    mine = lax.dynamic_index_in_dim(parts, core, 1, keepdims=False)
    other, mine = hold((other, mine))
    other = lax.ppermute(other, "col", [(i, i ^ 1) for i in range(4)])
    pair = mine.astype(jnp.float32) + other.astype(jnp.float32)
    away = pick(pair, 1 - x).astype(jnp.bfloat16)
    away = lax.ppermute(away, "col", [(i, i ^ 2) for i in range(4)])
    return pick(pair, x) + away.astype(jnp.float32)


def shards(gate_pre, up_pre, out_grad, down_weight):
    gate32 = gate_pre.astype(jnp.float32)
    up32 = up_pre.astype(jnp.float32)
    sgate = jax.nn.sigmoid(gate32)
    act = gate32 * sgate
    hidden = hold((act * up32).astype(jnp.bfloat16))
    me = lax.axis_index("col")
    ahead = lax.ppermute(hidden, "col", [(i, i ^ 2) for i in range(4)])
    grad_apart = gather_apart(out_grad)
    grad_all = gather_near(grad_apart)
    ahead, grad_late = hold((ahead, grad_apart))
    pair = jnp.stack([lax.select_n(me >> 1, hidden, ahead), lax.select_n(me >> 1, ahead, hidden)])
    beside = lax.ppermute(pair, "col", [(i, i ^ 1) for i in range(4)])
    hidden_all = jnp.stack([lax.select_n(me & 1, pair, beside), lax.select_n(me & 1, beside, pair)], axis=1)
    hidden_all = hidden_all.reshape(-1, hidden.shape[1])
    layer_parts = jnp.dot(hidden_all, down_weight, preferred_element_type=jnp.float32).astype(jnp.bfloat16)
    layer_out = sum_over_row(layer_parts).astype(jnp.bfloat16)

    hidden_all, grad_all = hold((hidden_all, grad_all))
    factor = 1.0 / (hidden_all.shape[0] * lax.axis_size("dp")) ** 0.5
    local_grad = (
        lax.dot_general(
            hidden_all, grad_all, (((0,), (0,)), ((), ())), preferred_element_type=jnp.float32
        )
        * factor
    ).astype(jnp.bfloat16)
    local_grad, grad_late = hold((local_grad, grad_all))
    weight_grad = sum_over_dp(local_grad)
    back = lax.dot_general(
        grad_late, down_weight, (((1,), (1,)), ((), ())), preferred_element_type=jnp.float32
    ).astype(jnp.bfloat16)
    dhidden = sum_over_col(back)
    up_grad = (dhidden * act).astype(jnp.bfloat16)
    gate_grad = (dhidden * up32 * sgate * (1.0 + gate32 * (1.0 - sgate))).astype(jnp.bfloat16)
    return (layer_out, gate_grad, up_grad, weight_grad)


def solution(mesh):
    return jax.shard_map(
        shards,
        mesh=mesh,
        in_specs=(
            P(("dp", "col"), "row"),
            P(("dp", "col"), "row"),
            P(("dp", "row"), "col"),
            P("row", "col"),
        ),
        out_specs=(
            P(("dp", "row"), "col"),
            P(("dp", "col"), "row"),
            P(("dp", "col"), "row"),
            P(("row", "dp"), "col"),
        ),
        check_vma=False,
    )
```

```python
import jax
import jax.numpy as jnp
from jax import lax
from jax.sharding import PartitionSpec as P

hold = lax.optimization_barrier


def shifted(array, axis, by):
    count = lax.axis_size(axis)
    return lax.ppermute(array, axis, [(i, (i + by) % count) for i in range(count)])


def pick(array, index):
    return lax.dynamic_index_in_dim(array, index, 0, keepdims=False)


def gather_apart(block):
    groups = [[k, k + 4, k + 8, k + 12] for k in range(4)]
    return lax.all_gather(block, "row", axis=0, tiled=False, axis_index_groups=groups)


def two_away(array):
    rows, cols = lax.axis_size("row"), lax.axis_size("col")
    route = [
        (r * cols + c, (r + (2 if c % 2 == 0 else -2)) % rows * cols + c) for r in range(rows) for c in range(cols)
    ]
    return lax.ppermute(array, ("row", "col"), route)


def gather_near(same):
    low = lax.axis_index("row") & 3
    sets = [same]
    for by in (1, 2, 15):
        sets.append(two_away(same) if by == 2 else shifted(same, "row", by))
    whole = [lax.select_n((low - k) & 3, *sets) for k in range(4)]
    return jnp.stack(whole, axis=1).reshape(-1, same.shape[-1])


def sum_over_row(parts):
    count = lax.axis_size("row")
    parts = parts.reshape((count, parts.shape[0] // count) + parts.shape[1:])
    parts = lax.all_to_all(parts, "row", 0, 0, tiled=True)
    return jnp.sum(parts.astype(jnp.float32), axis=0)


def sum_over_dp(parts):
    parts = parts.reshape((4, 2, parts.shape[0] // 8) + parts.shape[1:])
    me = lax.axis_index("dp")
    y, x = me >> 1, me & 1
    own, *blocks = hold([pick(parts, (y + dy) & 3) for dy in (0, 2, 1, 3)])
    total = own.astype(jnp.float32)
    for dy, mine in zip((2, 1, 3), blocks):
        got = lax.ppermute(mine, "dp", [(i, (i + 2 * dy) % 8) for i in range(8)])
        total = total + got.astype(jnp.float32)
    away = pick(total, 1 - x).astype(jnp.bfloat16)
    away = lax.ppermute(away, "dp", [(i, i ^ 1) for i in range(8)])
    return pick(total, x) + away.astype(jnp.float32)


def sum_over_col(parts):
    parts = parts.reshape((2, 2, parts.shape[0] // 4) + parts.shape[1:])
    me = lax.axis_index("col")
    x, core = me >> 1, me & 1
    other = lax.dynamic_index_in_dim(parts, 1 - core, 1, keepdims=False)
    mine = lax.dynamic_index_in_dim(parts, core, 1, keepdims=False)
    other, mine = hold((other, mine))
    other = lax.ppermute(other, "col", [(i, i ^ 1) for i in range(4)])
    pair = mine.astype(jnp.float32) + other.astype(jnp.float32)
    away = pick(pair, 1 - x).astype(jnp.bfloat16)
    away = lax.ppermute(away, "col", [(i, i ^ 2) for i in range(4)])
    return pick(pair, x) + away.astype(jnp.float32)


def shards(gate_pre, up_pre, out_grad, down_weight):
    gate32 = gate_pre.astype(jnp.float32)
    up32 = up_pre.astype(jnp.float32)
    sgate = jax.nn.sigmoid(gate32)
    act = gate32 * sgate
    hidden = hold((act * up32).astype(jnp.bfloat16))
    me = lax.axis_index("col")
    ahead = lax.ppermute(hidden, "col", [(i, i ^ 2) for i in range(4)])
    grad_apart = gather_apart(out_grad)
    grad_all = gather_near(grad_apart)
    ahead, grad_late = hold((ahead, grad_apart))
    pair = jnp.stack([lax.select_n(me >> 1, hidden, ahead), lax.select_n(me >> 1, ahead, hidden)])
    beside = lax.ppermute(pair, "col", [(i, i ^ 1) for i in range(4)])
    hidden_all = jnp.stack([lax.select_n(me & 1, pair, beside), lax.select_n(me & 1, beside, pair)], axis=1)
    hidden_all = hidden_all.reshape(-1, hidden.shape[1])
    layer_parts = jnp.dot(hidden_all, down_weight, preferred_element_type=jnp.float32).astype(jnp.bfloat16)
    layer_out = sum_over_row(layer_parts).astype(jnp.bfloat16)

    hidden_all, grad_all = hold((hidden_all, grad_all))
    factor = 1.0 / (hidden_all.shape[0] * lax.axis_size("dp")) ** 0.5
    local_grad = (
        lax.dot_general(
            hidden_all, grad_all, (((0,), (0,)), ((), ())), preferred_element_type=jnp.float32
        )
        * factor
    ).astype(jnp.bfloat16)
    local_grad, grad_late = hold((local_grad, grad_all))
    weight_grad = sum_over_dp(local_grad)
    back = lax.dot_general(
        grad_late, down_weight, (((1,), (1,)), ((), ())), preferred_element_type=jnp.float32
    ).astype(jnp.bfloat16)
    dhidden = sum_over_col(back)
    up_grad = (dhidden * act).astype(jnp.bfloat16)
    gate_grad = (dhidden * up32 * sgate * (1.0 + gate32 * (1.0 - sgate))).astype(jnp.bfloat16)
    return (layer_out, gate_grad, up_grad, weight_grad)


def solution(mesh):
    return jax.shard_map(
        shards,
        mesh=mesh,
        in_specs=(
            P(("dp", "col"), "row"),
            P(("dp", "col"), "row"),
            P(("dp", "row"), "col"),
            P("row", "col"),
        ),
        out_specs=(
            P(("dp", "row"), "col"),
            P(("dp", "col"), "row"),
            P(("dp", "col"), "row"),
            P(("row", "dp"), "col"),
        ),
        check_vma=False,
    )
```

```python
import jax
import jax.numpy as jnp
from jax import lax
from jax.sharding import PartitionSpec as P

hold = lax.optimization_barrier


def shifted(array, axis, by):
    count = lax.axis_size(axis)
    return lax.ppermute(array, axis, [(i, (i + by) % count) for i in range(count)])


def pick(array, index):
    return lax.dynamic_index_in_dim(array, index, 0, keepdims=False)


def gather_apart(block):
    groups = [[k, k + 4, k + 8, k + 12] for k in range(4)]
    return lax.all_gather(block, "row", axis=0, tiled=False, axis_index_groups=groups)


def two_away(array):
    rows, cols = lax.axis_size("row"), lax.axis_size("col")
    route = [
        (r * cols + c, (r + (2 if c % 2 == 0 else -2)) % rows * cols + c) for r in range(rows) for c in range(cols)
    ]
    return lax.ppermute(array, ("row", "col"), route)


def gather_near(same):
    sets = [same]
    for by in (1, 2, 15):
        sets.append(two_away(same) if by == 2 else shifted(same, "row", by))
    return sets


def assemble(sets, low):
    same = sets[0]
    whole = [lax.select_n((low - k) & 3, *sets) for k in range(4)]
    return jnp.stack(whole, axis=1).reshape(-1, same.shape[-1])


def pair_rows(parts):
    parts = parts.reshape((8, 2, parts.shape[0] // 16) + parts.shape[1:])
    parity = lax.axis_index("row") & 1
    other = lax.dynamic_index_in_dim(parts, 1 - parity, 1, keepdims=False)
    mine = lax.dynamic_index_in_dim(parts, parity, 1, keepdims=False)
    other, mine = hold((other, mine))
    other = lax.ppermute(other, "row", [(i, i ^ 1) for i in range(lax.axis_size("row"))])
    return (mine.astype(jnp.float32) + other.astype(jnp.float32)).astype(jnp.bfloat16)


def sum_over_row(parts):
    groups = [list(range(0, 16, 2)), list(range(1, 16, 2))]
    parts = lax.all_to_all(parts, "row", 0, 0, tiled=True, axis_index_groups=groups)
    return jnp.sum(parts.astype(jnp.float32), axis=0)


def sum_over_dp(parts):
    parts = parts.reshape((4, 2, parts.shape[0] // 8) + parts.shape[1:])
    me = lax.axis_index("dp")
    y, x = me >> 1, me & 1
    own, *blocks = hold([pick(parts, (y + dy) & 3) for dy in (0, 2, 1, 3)])
    total = own.astype(jnp.float32)
    for dy, mine in zip((2, 1, 3), blocks):
        got = lax.ppermute(mine, "dp", [(i, (i + 2 * dy) % 8) for i in range(8)])
        total = total + got.astype(jnp.float32)
    away = pick(total, 1 - x).astype(jnp.bfloat16)
    away = lax.ppermute(away, "dp", [(i, i ^ 1) for i in range(8)])
    return pick(total, x) + away.astype(jnp.float32)


def sum_over_col(parts):
    parts = parts.reshape((2, 2, parts.shape[0] // 4) + parts.shape[1:])
    me = lax.axis_index("col")
    x, core = me >> 1, me & 1
    other = lax.dynamic_index_in_dim(parts, 1 - core, 1, keepdims=False)
    mine = lax.dynamic_index_in_dim(parts, core, 1, keepdims=False)
    other, mine = hold((other, mine))
    other = lax.ppermute(other, "col", [(i, i ^ 1) for i in range(4)])
    pair = mine.astype(jnp.float32) + other.astype(jnp.float32)
    away = pick(pair, 1 - x).astype(jnp.bfloat16)
    away = lax.ppermute(away, "col", [(i, i ^ 2) for i in range(4)])
    return pick(pair, x) + away.astype(jnp.float32)


def shards(gate_pre, up_pre, out_grad, down_weight):
    gate32 = gate_pre.astype(jnp.float32)
    up32 = up_pre.astype(jnp.float32)
    sgate = jax.nn.sigmoid(gate32)
    act = gate32 * sgate
    hidden = hold((act * up32).astype(jnp.bfloat16))
    me = lax.axis_index("col")
    ahead = lax.ppermute(hidden, "col", [(i, i ^ 2) for i in range(4)])
    grad_apart = gather_apart(out_grad)
    sets = gather_near(grad_apart)
    ahead, grad_late = hold((ahead, grad_apart))
    pair = jnp.stack([lax.select_n(me >> 1, hidden, ahead), lax.select_n(me >> 1, ahead, hidden)])
    beside = lax.ppermute(pair, "col", [(i, i ^ 1) for i in range(4)])
    hidden_all = jnp.stack([lax.select_n(me & 1, pair, beside), lax.select_n(me & 1, beside, pair)], axis=1)
    hidden_all = hidden_all.reshape(-1, hidden.shape[1])
    layer_parts = jnp.dot(hidden_all, down_weight, preferred_element_type=jnp.float32).astype(jnp.bfloat16)
    layer_parts, low = hold((layer_parts, lax.axis_index("row") & 3))
    grad_all = assemble(sets, low)
    layer_out = sum_over_row(pair_rows(layer_parts)).astype(jnp.bfloat16)

    hidden_all, grad_all = hold((hidden_all, grad_all))
    factor = 1.0 / (hidden_all.shape[0] * lax.axis_size("dp")) ** 0.5
    local_grad = (
        lax.dot_general(
            hidden_all, grad_all, (((0,), (0,)), ((), ())), preferred_element_type=jnp.float32
        )
        * factor
    ).astype(jnp.bfloat16)
    local_grad, grad_late = hold((local_grad, grad_all))
    weight_grad = sum_over_dp(local_grad)
    back = lax.dot_general(
        grad_late, down_weight, (((1,), (1,)), ((), ())), preferred_element_type=jnp.float32
    ).astype(jnp.bfloat16)
    dhidden = sum_over_col(back)
    up_grad = (dhidden * act).astype(jnp.bfloat16)
    gate_grad = (dhidden * up32 * sgate * (1.0 + gate32 * (1.0 - sgate))).astype(jnp.bfloat16)
    return (layer_out, gate_grad, up_grad, weight_grad)


def solution(mesh):
    return jax.shard_map(
        shards,
        mesh=mesh,
        in_specs=(
            P(("dp", "col"), "row"),
            P(("dp", "col"), "row"),
            P(("dp", "row"), "col"),
            P("row", "col"),
        ),
        out_specs=(
            P(("dp", "row"), "col"),
            P(("dp", "col"), "row"),
            P(("dp", "col"), "row"),
            P(("row", "dp"), "col"),
        ),
        check_vma=False,
    )
```
